128 devices in a mesh: row: 16 (over x, y), col: 8 (over z, core).
Axes of the slice: x: 4, y: 4, z: 4, core: 2. Of those that a mesh axis runs over, the one named last changes fastest.
Arguments:
- features: float32 [32768, 256], P(('row', 'col')), may hold values from -6 to 6
- new_features: float32 [8192, 256], P(('row', 'col')), may hold values from -6 to 6
- lengths: int32 [32768], P(('row', 'col')), may hold values from 1 to 64
- targets: float32 [32768, 64], P(('row', 'col')), may hold values from -6 to 6
- prior_train: float32 [32768, 256], P(('row', 'col')), may hold values from -6 to 6
- noise_draw: float32 [32768, 256], P(('row', 'col')), may hold values from -6 to 6
- prior_new: float32 [8192, 256], P(('row', 'col')), may hold values from -6 to 6
- time_kernel: float32 [64, 64], replicated, may hold values from -16 to 16.5, as said below
- noise_var: float32 [64], replicated, may hold values from 0.05 to 0.5
Outputs:
- residual: float32 [32768, 256], P(('row', 'col'))
- predicted: float32 [8192, 256], P(('row', 'col'))
The draws below stay inside these ranges and needn't reach their ends.
Inputs may be any that keep to these rules, and one draw needn't show every extreme that they name: `time_kernel`: symmetric positive definite.
All inputs are finite; a program needn't handle non-finite values.
Results may differ from the reference program's by a relative error of at most 0.00022.
Values sent between devices are 32-bit elements; how exact they have to be, the bound alone decides.
No kernel may reach another device: no remote copies, remote signals or barrier semaphores. Data moves between devices by JAX's collectives and lax.ppermute only.
A program may use at most 128 MiB of HBM per device.

```python
import math
import jax
import jax.numpy as jnp
from jax import lax

FEATURES = 256
CHECKPOINTS = 64
SAMPLES = 4
ITERS = 2
ITEMS = 32768
NEW_ITEMS = 8192
N_ROW = 16


def draw_time_kernel(key, part):
    first = jax.random.fold_in(jax.random.fold_in(key, 17), 0)
    base = jnp.clip(jax.random.normal(first, (CHECKPOINTS, CHECKPOINTS), jnp.float32), -4.0, 4.0)
    gram = jnp.dot(base, base.T, precision=lax.Precision.HIGHEST) / CHECKPOINTS
    return gram + 0.5 * jnp.eye(CHECKPOINTS, dtype=jnp.float32)


def plant(values, rng, smallest, high):
    longest = values.shape.index(max(values.shape))
    spots = []
    for shift in (0, 1):
        where = [jax.random.randint(jax.random.fold_in(rng, axis), (), 0, length) for axis, length in enumerate(values.shape)]
        where[longest] = (where[longest] + shift) % values.shape[longest]
        spots.append(tuple(where))
    return values.at[spots[0]].set(smallest).at[spots[1]].set(high)


def shard_levels(key, dims, cuts, least, high):
    level = 1.0
    for axis_at, shards_of in cuts:
        steps = jax.random.uniform(jax.random.fold_in(jax.random.fold_in(key, 6), axis_at), (shards_of,), jnp.float32, least / len(cuts), high / len(cuts))
        level = level * jnp.repeat(jnp.exp(steps), dims[axis_at] // shards_of).reshape((-1,) + (1,) * (len(dims) - 1 - axis_at))
    return level


def noise(stream_key, extent, deviation, reach, pieces=(), kind=jnp.bfloat16):
    gain = shard_levels(stream_key, extent, pieces, -0.22, 0.18) if pieces else 1.0
    values = jax.random.normal(stream_key, extent, jnp.float32) * deviation * gain
    return jnp.minimum(jnp.maximum(values, -reach), reach).astype(kind)


def setup_inputs(seed: int = 0) -> dict:
    streams_of = jax.random.split(jax.random.key(seed), 10)
    return {
        "features": noise(streams_of[0], (ITEMS, FEATURES), 1.0, 6.0, ((0, 128),), jnp.float32),
        "new_features": noise(streams_of[1], (NEW_ITEMS, FEATURES), 1.0, 6.0, ((0, 128),), jnp.float32),
        "lengths": plant(jax.random.randint(streams_of[2], (ITEMS,), 1, CHECKPOINTS + 1), jax.random.fold_in(streams_of[2], 1), 1, CHECKPOINTS).astype(jnp.int32),
        "targets": noise(streams_of[3], (ITEMS, CHECKPOINTS), 1.0, 6.0, ((0, 128),), jnp.float32),
        "prior_train": noise(streams_of[4], (ITEMS, SAMPLES * CHECKPOINTS), 1.0, 6.0, ((0, 128),), jnp.float32),
        "noise_draw": noise(streams_of[5], (ITEMS, SAMPLES * CHECKPOINTS), 1.0, 6.0, ((0, 128),), jnp.float32),
        "prior_new": noise(streams_of[6], (NEW_ITEMS, SAMPLES * CHECKPOINTS), 1.0, 6.0, ((0, 128),), jnp.float32),
        "time_kernel": draw_time_kernel(jax.random.fold_in(streams_of[9], 71), 0),
        "noise_var": jnp.clip(jnp.exp(jax.random.uniform(streams_of[8], (CHECKPOINTS,), jnp.float32, math.log(0.05), math.log(0.5))), 0.05, 0.5),
    }


def unit_rows(values):
    return values / jnp.sqrt(lax.optimization_barrier(jnp.sum(values * values, axis=1, keepdims=True)) + 1e-06)

def kernel(left, right):
    inner = lax.dot_general(left, right, (((1,), (1,)), ((), ())), precision=lax.Precision.HIGHEST)
    return inner + inner * inner * inner

def kernel_apply(left, right, values):
    blocks = left.reshape(N_ROW, -1, left.shape[1])

    def one_block(block):
        return jnp.dot(kernel(block, right), values, precision=lax.Precision.HIGHEST)
    return lax.map(one_block, blocks).reshape(-1, values.shape[1])

def reference(features, new_features, lengths, targets, prior_train, noise_draw, prior_new, time_kernel, noise_var):
    normed = unit_rows(features)
    normed_new = unit_rows(new_features)
    mixing = jnp.kron(jnp.eye(SAMPLES, dtype=time_kernel.dtype), time_kernel)
    position = jnp.arange(SAMPLES * CHECKPOINTS, dtype=jnp.int32) % CHECKPOINTS
    mask = (position[None, :] < lengths[:, None]).astype(targets.dtype)
    noise_cols = jnp.tile(noise_var, SAMPLES)
    rhs = mask * (jnp.tile(targets, (1, SAMPLES)) - prior_train - jnp.sqrt(noise_cols) * noise_draw)

    def operate(direction):
        mixed = jnp.dot(direction, mixing, precision=lax.Precision.HIGHEST)
        return mask * kernel_apply(normed, normed, mixed) + noise_cols * direction

    def per_sample(first, second):
        return lax.optimization_barrier(jnp.sum((first * second).reshape(first.shape[0], SAMPLES, CHECKPOINTS), axis=(0, 2)))
    solution = jnp.zeros_like(rhs)
    residual = rhs
    direction = rhs
    norm_now = per_sample(residual, residual)
    for step in range(ITERS):
        image = operate(direction)
        alpha = jnp.repeat(norm_now / per_sample(direction, image), CHECKPOINTS)
        solution = solution + alpha * direction
        residual = residual - alpha * image
        if step + 1 < ITERS:
            norm_next = per_sample(residual, residual)
            direction = residual + jnp.repeat(norm_next / norm_now, CHECKPOINTS) * direction
            norm_now = norm_next
    mixed_solution = jnp.dot(solution, mixing, precision=lax.Precision.HIGHEST)
    predicted = prior_new + kernel_apply(normed_new, normed, mixed_solution)
    return (residual, predicted)
```

```python
import jax
import jax.numpy as jnp
from jax import lax
from jax.experimental import pallas as pl
from jax.experimental.pallas import tpu as pltpu
from jax.sharding import PartitionSpec as P


AXES = ("row", "col")
F32 = jnp.float32
BF16 = jnp.bfloat16


def index(x, y, z, core):
    return ((x % 4) * 4 + y % 4) * 8 + (z % 4) * 2 + core % 2


def shift(values, dx=0, dy=0, dz=0, core=0):
    pairs = [
        (index(x, y, z, k), index(x + dx, y + dy, z + dz, k + core))
        for x in range(4)
        for y in range(4)
        for z in range(4)
        for k in range(2)
    ]
    return lax.ppermute(values, AXES, pairs)


def ring(values, axis):
    half = values.shape[0] // 2
    below = shift(values, **{axis: 1})
    above = shift(values, **{axis: -1})
    first = shift(below[:half], **{axis: 1})
    second = shift(above[half:], **{axis: -1})
    return [values, below, above, first, second]


def join_kernel(*refs):
    start = 0
    for ref in refs[:-1]:
        refs[-1][start : start + ref.shape[0], :] = ref[...]
        start += ref.shape[0]


def join(parts):
    rows = sum(part.shape[0] for part in parts)
    return pl.pallas_call(
        join_kernel,
        out_shape=jax.ShapeDtypeStruct((rows, parts[0].shape[1]), F32),
        name="join",
    )(*parts)


def plane_half(values, near, far):
    return ring(join(ring(values, near)), far)


def plane_gather(values):
    middle = values.shape[0] // 2
    return [plane_half(values[:middle], "dx", "dy"), plane_half(values[middle:], "dy", "dx")]


OFFSETS = (0, -1, 1, 2)


def plane_order():
    row = lax.axis_index("row")
    x, y = row // 4, row % 4
    steps = [(near, far) for far in OFFSETS for near in OFFSETS]
    one = [(((x + 4 + near) % 4) * 4 + (y + 4 + far) % 4) * 2 for near, far in steps]
    two = [(((x + 4 + far) % 4) * 4 + (y + 4 + near) % 4) * 2 + 1 for near, far in steps]
    return jnp.stack(one + two).astype(jnp.int32)


def line_order(other):
    col = lax.axis_index("col")
    z, core = col // 2, (col + other) % 2
    return jnp.stack([((z + 4 + step) % 4) * 2 + core for step in OFFSETS]).astype(jnp.int32)


def split(values):
    high = values.astype(BF16)
    return high, (values - high.astype(F32)).astype(BF16)


def dot(first, second, dims=(((1,), (0,)), ((), ()))):
    return lax.dot_general(first, second, dims, preferred_element_type=F32)


def dot_split(first, second, dims=(((1,), (0,)), ((), ()))):
    return dot(first[0], second[0], dims) + (
        dot(first[0], second[1], dims) + dot(first[1], second[0], dims)
    )


def form_kernel(n, order, *refs):
    cols, rows, high_out, low_out, high_cols, low_cols, high_rows, low_rows = refs[:n], *refs[n:]
    step = pl.program_id(0)

    @pl.when(step == 0)
    def _():
        start = 0
        for ref in cols:
            high, low = split(ref[...])
            high_cols[start : start + ref.shape[0], :] = high
            low_cols[start : start + ref.shape[0], :] = low
            start += ref.shape[0]
        size = rows.shape[1]
        for i in range(4):
            high, low = split(rows[order[i]])
            high_rows[i * size : (i + 1) * size, :] = high
            low_rows[i * size : (i + 1) * size, :] = low

    width = high_out.shape[1]
    here = pl.ds(pl.multiple_of(step * width, width), width)
    inner = dot_split(
        (high_rows[...], low_rows[...]),
        (high_cols[here, :], low_cols[here, :]),
        (((1,), (1,)), ((), ())),
    )
    high, low = split(inner + inner * inner * inner)
    high_out[...] = high
    low_out[...] = low


def whole(part):
    return pl.BlockSpec(part.shape, lambda i, *_: (0,) * part.ndim)


def form(order, rows, cols, block):
    width = sum(part.shape[0] for part in cols)
    total, depth = 4 * rows.shape[1], rows.shape[2]
    tile = pl.BlockSpec((total, block), lambda i, *_: (0, i))
    return pl.pallas_call(
        lambda *refs: form_kernel(len(cols), *refs),
        grid_spec=pltpu.PrefetchScalarGridSpec(
            num_scalar_prefetch=1,
            grid=(width // block,),
            in_specs=[whole(part) for part in [*cols, rows]],
            out_specs=[tile, tile],
            scratch_shapes=[pltpu.VMEM((width, depth), BF16)] * 2
            + [pltpu.VMEM((total, depth), BF16)] * 2,
        ),
        out_shape=[jax.ShapeDtypeStruct((total, width), BF16)] * 2,
        cost_estimate=pl.CostEstimate(
            flops=6 * total * width * depth, bytes_accessed=4 * total * width, transcendentals=0
        ),
        name="form",
    )(order, *cols, rows)


def apply_kernel(n, order, values, *refs):
    tests, high_tile, low_tile, out, sums = refs[:n], *refs[n:]
    step = pl.program_id(0)
    count = high_tile.shape[1] // values.shape[1]
    part = jnp.concatenate([values[order[step * count + i]] for i in range(count)], axis=0)
    result = dot_split((high_tile[...], low_tile[...]), split(part))

    @pl.when(step == 0)
    def _():
        out[...] = result

    @pl.when(step > 0)
    def _():
        out[...] += result

    @pl.when(step == pl.num_programs(0) - 1)
    def _():
        sums[...] = jnp.zeros_like(sums)
        for j, test in enumerate(tests):
            size, block = test.shape[0] // 4, out.shape[0] // 4
            for i in range(4):
                product = test[i * size : (i + 1) * size, :] * out[i * block : i * block + size, :]
                sums[j : j + 1, :] += jnp.sum(product, axis=0, keepdims=True)


def apply(tile, block, order, values, *tests):
    total, width = tile[0].shape
    columns = values.shape[2]
    tiles = pl.BlockSpec((total, block), lambda i, *_: (0, i))
    out_shape = [
        jax.ShapeDtypeStruct((total, columns), F32),
        jax.ShapeDtypeStruct((8, columns), F32),
    ]
    return pl.pallas_call(
        lambda *refs: apply_kernel(len(tests), *refs),
        grid_spec=pltpu.PrefetchScalarGridSpec(
            num_scalar_prefetch=1,
            grid=(width // block,),
            in_specs=[whole(part) for part in [values, *tests]] + [tiles, tiles],
            out_specs=[whole(part) for part in out_shape],
        ),
        out_shape=out_shape,
        cost_estimate=pl.CostEstimate(
            flops=6 * total * width * columns, bytes_accessed=4 * total * width, transcendentals=0
        ),
        name="apply",
    )(order, values, *tests, *tile)


def total_sums(partial, samples):
    devices = lax.axis_size("row") * lax.axis_size("col")
    spread = jnp.broadcast_to(partial[None], (devices,) + partial.shape)
    sums = jnp.sum(lax.all_to_all(spread, AXES, 0, 0), axis=0)
    return jnp.sum(sums.reshape(partial.shape[0], samples, -1), axis=2)


def shards(
    features,
    new_features,
    lengths,
    targets,
    prior_train,
    noise_draw,
    prior_new,
    time_kernel,
    noise_var,
):
    checkpoints = time_kernel.shape[0]
    columns = prior_train.shape[1]
    samples = columns // checkpoints
    items = features.shape[0]
    block = items + new_features.shape[0]

    both = jnp.concatenate([features, new_features], axis=0)
    normed = both / jnp.sqrt(jnp.sum(both * both, axis=1, keepdims=True) + 1e-06)

    line = lax.axis_size("col")
    rows = lax.all_to_all(jnp.broadcast_to(normed[None], (line,) + normed.shape), "col", 0, 0)
    cols = [part for half in plane_gather(normed[:items]) for part in half]
    middle = block // 2

    mixing = jnp.kron(jnp.eye(samples, dtype=F32), time_kernel)

    def mix(values):
        return jnp.dot(values, mixing, precision=lax.Precision.HIGHEST)

    position = jnp.arange(columns, dtype=jnp.int32) % checkpoints
    mask = (position[None, :] < lengths[:, None]).astype(F32)
    noise_cols = jnp.tile(noise_var, samples)
    rhs = mask * (jnp.tile(targets, (1, samples)) - prior_train - jnp.sqrt(noise_cols) * noise_draw)
    plane = lax.axis_size("row")
    order = plane_order()

    def exchange(values):
        spread_out = jnp.broadcast_to(values[None], (plane, items, columns))
        received = lax.all_to_all(spread_out, "row", 0, 0)
        return received.reshape(2 * plane, items // 2, columns)

    def line_gather(values):
        own = join(ring(values, "dz"))
        return own, shift(own, core=1)

    def reduce_rows(own, other):
        received = shift(other, core=1)
        own, below, above, opposite = jnp.split(own + received, 4)
        up = shift(opposite[:middle], dz=1)
        down = shift(opposite[middle:], dz=-1)
        above = jnp.concatenate([above[:middle] + up, above[middle:]], axis=0)
        below = jnp.concatenate([below[:middle], below[middle:] + down], axis=0)
        own = own + (shift(above, dz=1) + shift(below, dz=-1))
        return own[:items], own[items:]

    def spread(scalars):
        return jnp.repeat(scalars, checkpoints)[None, :]

    def local_sums(*pairs):
        return [jnp.sum(first * second, axis=0) for first, second in pairs]

    mixed = exchange(mix(rhs))
    rhs_own, rhs_other = line_gather(rhs)
    tile_other = form(line_order(1), rows, cols, 256)
    tile_own = form(line_order(0), rows, cols, 256)
    other, sums_other = apply(tile_other, 1024, order, mixed, rhs_other)
    own, sums_own = apply(tile_own, 1024, order, mixed, rhs_own)
    norm_first, noise_first = local_sums((rhs, rhs), (rhs, noise_cols * rhs))
    curve_first = sums_own[0] + sums_other[0] + noise_first
    norm_first, curve_first = total_sums(jnp.stack([norm_first, curve_first]), samples)
    train, new_first = reduce_rows(own, other)
    image = mask * train + noise_cols * rhs
    step_first = norm_first / curve_first
    residual = rhs - spread(step_first) * image

    mixed = exchange(mix(residual))
    res_own, res_other = line_gather(residual)
    other, sums_other = apply(tile_other, 1024, order, mixed, rhs_other, res_other)
    own, sums_own = apply(tile_own, 1024, order, mixed, rhs_own, res_own)
    tests = sums_own + sums_other
    norm_next, res_image, noise_rhs, noise_res = local_sums(
        (residual, residual),
        (residual, image),
        (rhs, noise_cols * residual),
        (residual, noise_cols * residual),
    )
    partial = jnp.stack([norm_next, res_image, tests[0] + noise_rhs, tests[1] + noise_res])
    norm_next, res_image, rhs_answer, res_answer = total_sums(partial, samples)
    ratio = norm_next / norm_first
    curve_second = res_answer + ratio * (res_image + rhs_answer + ratio * curve_first)
    step_second = norm_next / curve_second
    train, new_second = reduce_rows(own, other)
    answer = mask * train + noise_cols * residual
    residual = residual - spread(step_second) * (answer + spread(ratio) * image)
    predicted = (
        prior_new
        + spread(step_first + step_second * ratio) * new_first
        + spread(step_second) * new_second
    )
    return (residual, predicted)


def solution(mesh):
    return jax.shard_map(
        shards,
        mesh=mesh,
        in_specs=(
            P(("row", "col"), None),
            P(("row", "col"), None),
            P(("row", "col")),
            P(("row", "col"), None),
            P(("row", "col"), None),
            P(("row", "col"), None),
            P(("row", "col"), None),
            P(),
            P(),
        ),
        out_specs=(P(("row", "col"), None), P(("row", "col"), None)),
        check_vma=False,
    )
```

```python
import jax
import jax.numpy as jnp
from jax import lax
from jax.experimental import pallas as pl
from jax.experimental.pallas import tpu as pltpu
from jax.sharding import PartitionSpec as P


AXES = ("row", "col")
F32 = jnp.float32
BF16 = jnp.bfloat16


def index(x, y, z, core):
    return ((x % 4) * 4 + y % 4) * 8 + (z % 4) * 2 + core % 2


def shift(values, dx=0, dy=0, dz=0, core=0):
    pairs = [
        (index(x, y, z, k), index(x + dx, y + dy, z + dz, k + core))
        for x in range(4)
        for y in range(4)
        for z in range(4)
        for k in range(2)
    ]
    return lax.ppermute(values, AXES, pairs)


def ring(values, axis):
    half = values.shape[0] // 2
    below = shift(values, **{axis: 1})
    above = shift(values, **{axis: -1})
    first = shift(below[:half], **{axis: 1})
    second = shift(above[half:], **{axis: -1})
    return [values, below, above, first, second]


def join_kernel(*refs):
    start = 0
    for ref in refs[:-1]:
        refs[-1][start : start + ref.shape[0], :] = ref[...]
        start += ref.shape[0]


def join(parts):
    rows = sum(part.shape[0] for part in parts)
    return pl.pallas_call(
        join_kernel,
        out_shape=jax.ShapeDtypeStruct((rows, parts[0].shape[1]), F32),
        name="join",
    )(*parts)


def plane_half(values, near, far):
    return ring(join(ring(values, near)), far)


def plane_gather(values):
    middle = values.shape[0] // 2
    return [plane_half(values[:middle], "dx", "dy"), plane_half(values[middle:], "dy", "dx")]


OFFSETS = (0, -1, 1, 2)


def plane_order():
    row = lax.axis_index("row")
    x, y = row // 4, row % 4
    steps = [(near, far) for far in OFFSETS for near in OFFSETS]
    one = [(((x + 4 + near) % 4) * 4 + (y + 4 + far) % 4) * 2 for near, far in steps]
    two = [(((x + 4 + far) % 4) * 4 + (y + 4 + near) % 4) * 2 + 1 for near, far in steps]
    return jnp.stack(one + two).astype(jnp.int32)


def line_order(other):
    col = lax.axis_index("col")
    z, core = col // 2, (col + other) % 2
    return jnp.stack([((z + 4 + step) % 4) * 2 + core for step in OFFSETS]).astype(jnp.int32)


def split(values):
    high = values.astype(BF16)
    return high, (values - high.astype(F32)).astype(BF16)


def dot(first, second, dims=(((1,), (0,)), ((), ()))):
    return lax.dot_general(first, second, dims, preferred_element_type=F32)


def dot_split(first, second, dims=(((1,), (0,)), ((), ()))):
    return dot(first[0], second[0], dims) + (
        dot(first[0], second[1], dims) + dot(first[1], second[0], dims)
    )


def form_kernel(n, order, *refs):
    cols, rows, high_out, low_out, high_cols, low_cols, high_rows, low_rows = refs[:n], *refs[n:]
    step = pl.program_id(0)

    @pl.when(step == 0)
    def _():
        start = 0
        for ref in cols:
            high, low = split(ref[...])
            high_cols[start : start + ref.shape[0], :] = high
            low_cols[start : start + ref.shape[0], :] = low
            start += ref.shape[0]
        size = rows.shape[1]
        for i in range(4):
            high, low = split(rows[order[i]])
            high_rows[i * size : (i + 1) * size, :] = high
            low_rows[i * size : (i + 1) * size, :] = low

    width = high_out.shape[1]
    here = pl.ds(pl.multiple_of(step * width, width), width)
    inner = dot_split(
        (high_rows[...], low_rows[...]),
        (high_cols[here, :], low_cols[here, :]),
        (((1,), (1,)), ((), ())),
    )
    high, low = split(inner + inner * inner * inner)
    high_out[...] = high
    low_out[...] = low


def whole(part):
    return pl.BlockSpec(part.shape, lambda i, *_: (0,) * part.ndim)


def form(order, rows, cols, block):
    width = sum(part.shape[0] for part in cols)
    total, depth = 4 * rows.shape[1], rows.shape[2]
    tile = pl.BlockSpec((total, block), lambda i, *_: (0, i))
    return pl.pallas_call(
        lambda *refs: form_kernel(len(cols), *refs),
        grid_spec=pltpu.PrefetchScalarGridSpec(
            num_scalar_prefetch=1,
            grid=(width // block,),
            in_specs=[whole(part) for part in [*cols, rows]],
            out_specs=[tile, tile],
            scratch_shapes=[pltpu.VMEM((width, depth), BF16)] * 2
            + [pltpu.VMEM((total, depth), BF16)] * 2,
        ),
        out_shape=[jax.ShapeDtypeStruct((total, width), BF16)] * 2,
        cost_estimate=pl.CostEstimate(
            flops=6 * total * width * depth, bytes_accessed=4 * total * width, transcendentals=0
        ),
        name="form",
    )(order, *cols, rows)


def apply_kernel(n, add, order, values, *refs):
    if add:
        before, refs = refs[0], refs[1:]
    tests, high_tile, low_tile, out, sums = refs[:n], *refs[n:]
    step = pl.program_id(0)
    count = high_tile.shape[1] // values.shape[1]
    part = jnp.concatenate([values[order[step * count + i]] for i in range(count)], axis=0)
    result = dot_split((high_tile[...], low_tile[...]), split(part))

    @pl.when(step == 0)
    def _():
        out[...] = result + before[...] if add else result

    @pl.when(step > 0)
    def _():
        out[...] += result

    @pl.when(step == pl.num_programs(0) - 1)
    def _():
        sums[...] = jnp.zeros_like(sums)
        for j, test in enumerate(tests):
            size, block = test.shape[0] // 4, out.shape[0] // 4
            for i in range(4):
                product = test[i * size : (i + 1) * size, :] * out[i * block : i * block + size, :]
                sums[j : j + 1, :] += jnp.sum(product, axis=0, keepdims=True)


def apply(tile, block, order, values, tests=(), before=None, start=0):
    total, columns = tile[0].shape[0], values.shape[2]
    width = order.shape[0] * values.shape[1]
    tiles = pl.BlockSpec((total, block), lambda i, *_: (0, start // block + i))
    operands = [values] + ([] if before is None else [before]) + list(tests)
    out_shape = [
        jax.ShapeDtypeStruct((total, columns), F32),
        jax.ShapeDtypeStruct((8, columns), F32),
    ]
    return pl.pallas_call(
        lambda *refs: apply_kernel(len(tests), before is not None, *refs),
        grid_spec=pltpu.PrefetchScalarGridSpec(
            num_scalar_prefetch=1,
            grid=(width // block,),
            in_specs=[whole(part) for part in operands] + [tiles, tiles],
            out_specs=[whole(part) for part in out_shape],
        ),
        out_shape=out_shape,
        cost_estimate=pl.CostEstimate(
            flops=6 * total * width * columns, bytes_accessed=4 * total * width, transcendentals=0
        ),
        name="apply",
    )(order, *operands, *tile)


def total_sums(partial, samples):
    devices = lax.axis_size("row") * lax.axis_size("col")
    spread = jnp.broadcast_to(partial[None], (devices,) + partial.shape)
    sums = jnp.sum(lax.all_to_all(spread, AXES, 0, 0), axis=0)
    return jnp.sum(sums.reshape(partial.shape[0], samples, -1), axis=2)


def shards(
    features,
    new_features,
    lengths,
    targets,
    prior_train,
    noise_draw,
    prior_new,
    time_kernel,
    noise_var,
):
    checkpoints = time_kernel.shape[0]
    columns = prior_train.shape[1]
    samples = columns // checkpoints
    items = features.shape[0]
    block = items + new_features.shape[0]

    both = jnp.concatenate([features, new_features], axis=0)
    normed = both / jnp.sqrt(jnp.sum(both * both, axis=1, keepdims=True) + 1e-06)

    line = lax.axis_size("col")
    rows = lax.all_to_all(jnp.broadcast_to(normed[None], (line,) + normed.shape), "col", 0, 0)
    cols = [part for half in plane_gather(normed[:items]) for part in half]
    middle = block // 2

    mixing = jnp.kron(jnp.eye(samples, dtype=F32), time_kernel)

    def mix(values):
        return jnp.dot(values, mixing, precision=lax.Precision.HIGHEST)

    position = jnp.arange(columns, dtype=jnp.int32) % checkpoints
    mask = (position[None, :] < lengths[:, None]).astype(F32)
    noise_cols = jnp.tile(noise_var, samples)
    rhs = mask * (jnp.tile(targets, (1, samples)) - prior_train - jnp.sqrt(noise_cols) * noise_draw)
    plane = lax.axis_size("row")
    order = plane_order()
    half = items // 2

    def exchange(values):
        spread_out = jnp.broadcast_to(values[None], (plane,) + values.shape)
        received = lax.all_to_all(spread_out, "row", 0, 0)
        return received.reshape(-1, half, columns)

    def line_gather(values):
        own = join(ring(values, "dz"))
        return own, shift(own, core=1)

    def reduce_rows(own, other):
        received = shift(other, core=1)
        own, below, above, opposite = jnp.split(own + received, 4)
        up = shift(opposite[:middle], dz=1)
        down = shift(opposite[middle:], dz=-1)
        above = jnp.concatenate([above[:middle] + up, above[middle:]], axis=0)
        below = jnp.concatenate([below[:middle], below[middle:] + down], axis=0)
        own = own + (shift(above, dz=1) + shift(below, dz=-1))
        return own[:items], own[items:]

    def spread(scalars):
        return jnp.repeat(scalars, checkpoints)[None, :]

    def local_sums(*pairs):
        return [jnp.sum(first * second, axis=0) for first, second in pairs]

    mixed = exchange(mix(rhs))
    rhs_own, rhs_other = line_gather(rhs)
    tile_other = form(line_order(1), rows, cols, 256)
    tile_own = form(line_order(0), rows, cols, 256)
    other, sums_other = apply(tile_other, 1024, order, mixed, [rhs_other])
    own, sums_own = apply(tile_own, 1024, order, mixed, [rhs_own])
    norm_first, noise_first = local_sums((rhs, rhs), (rhs, noise_cols * rhs))
    curve_first = sums_own[0] + sums_other[0] + noise_first
    norm_first, curve_first = total_sums(jnp.stack([norm_first, curve_first]), samples)
    train, new_first = reduce_rows(own, other)
    image = mask * train + noise_cols * rhs
    step_first = norm_first / curve_first
    residual = rhs - spread(step_first) * image

    start = mix(residual)
    mixed = [exchange(start[:half]), exchange(start[half:])]
    res_own, res_other = line_gather(residual)

    def second(tile, tests):
        orders = order.reshape(2, -1) // 2
        width = items * plane // 2
        result, _ = apply(tile, 1024, orders[0], mixed[0])
        return apply(tile, 1024, orders[1], mixed[1], tests, result, width)

    other, sums_other = second(tile_other, [rhs_other, res_other])
    own, sums_own = second(tile_own, [rhs_own, res_own])
    tests = sums_own + sums_other
    norm_next, res_image, noise_rhs, noise_res = local_sums(
        (residual, residual),
        (residual, image),
        (rhs, noise_cols * residual),
        (residual, noise_cols * residual),
    )
    partial = jnp.stack([norm_next, res_image, tests[0] + noise_rhs, tests[1] + noise_res])
    norm_next, res_image, rhs_answer, res_answer = total_sums(partial, samples)
    ratio = norm_next / norm_first
    curve_second = res_answer + ratio * (res_image + rhs_answer + ratio * curve_first)
    step_second = norm_next / curve_second
    train, new_second = reduce_rows(own, other)
    answer = mask * train + noise_cols * residual
    residual = residual - spread(step_second) * (answer + spread(ratio) * image)
    predicted = (
        prior_new
        + spread(step_first + step_second * ratio) * new_first
        + spread(step_second) * new_second
    )
    return (residual, predicted)


def solution(mesh):
    return jax.shard_map(
        shards,
        mesh=mesh,
        in_specs=(
            P(("row", "col"), None),
            P(("row", "col"), None),
            P(("row", "col")),
            P(("row", "col"), None),
            P(("row", "col"), None),
            P(("row", "col"), None),
            P(("row", "col"), None),
            P(),
            P(),
        ),
        out_specs=(P(("row", "col"), None), P(("row", "col"), None)),
        check_vma=False,
    )
```

```python
import jax
import jax.numpy as jnp
import numpy as np
from jax import lax
from jax.experimental import pallas as pl
from jax.experimental.pallas import tpu as pltpu
from jax.sharding import PartitionSpec as P


AXES = ("row", "col")
F32 = jnp.float32
BF16 = jnp.bfloat16


def index(x, y, z, core):
    return ((x % 4) * 4 + y % 4) * 8 + (z % 4) * 2 + core % 2


def shift(values, dx=0, dy=0, dz=0, core=0):
    pairs = [
        (index(x, y, z, k), index(x + dx, y + dy, z + dz, k + core))
        for x in range(4)
        for y in range(4)
        for z in range(4)
        for k in range(2)
    ]
    return lax.ppermute(values, AXES, pairs)


def ring(values, axis):
    half = values.shape[0] // 2
    below = shift(values, **{axis: 1})
    above = shift(values, **{axis: -1})
    first = shift(below[:half], **{axis: 1})
    second = shift(above[half:], **{axis: -1})
    return [values, below, above, first, second]


def join_kernel(*refs):
    start = 0
    for ref in refs[:-1]:
        refs[-1][start : start + ref.shape[0], :] = ref[...]
        start += ref.shape[0]


def join(parts):
    rows = sum(part.shape[0] for part in parts)
    return pl.pallas_call(
        join_kernel,
        out_shape=jax.ShapeDtypeStruct((rows, parts[0].shape[1]), F32),
        name="join",
    )(*parts)


def plane_half(values, near, far):
    return ring(join(ring(values, near)), far)


def plane_gather(values):
    middle = values.shape[0] // 2
    return [plane_half(values[:middle], "dx", "dy"), plane_half(values[middle:], "dy", "dx")]


OFFSETS = (0, -1, 1, 2)


def at(table, axis):
    return lax.dynamic_index_in_dim(jnp.asarray(table), lax.axis_index(axis), keepdims=False)


def plane_order():
    steps = [(near, far) for far in OFFSETS for near in OFFSETS]
    table = []
    for x in range(4):
        for y in range(4):
            one = [((x + near) % 4 * 4 + (y + far) % 4) * 2 for near, far in steps]
            two = [((x + far) % 4 * 4 + (y + near) % 4) * 2 + 1 for near, far in steps]
            table.append(one + two)
    return at(np.array(table, np.int32), "row")


def line_order(other):
    table = [
        [(z + step) % 4 * 2 + (core + other) % 2 for step in OFFSETS]
        for z in range(4)
        for core in range(2)
    ]
    return at(np.array(table, np.int32), "col")


def split(values):
    high = values.astype(BF16)
    return high, (values - high.astype(F32)).astype(BF16)


def dot(first, second, dims=(((1,), (0,)), ((), ()))):
    return lax.dot_general(first, second, dims, preferred_element_type=F32)


def dot_split(first, second, dims=(((1,), (0,)), ((), ()))):
    return dot(first[0], second[0], dims) + (
        dot(first[0], second[1], dims) + dot(first[1], second[0], dims)
    )


def form_kernel(n, order, *refs):
    cols, rows, high_out, low_out, high_cols, low_cols, high_rows, low_rows = refs[:n], *refs[n:]
    step = pl.program_id(0)

    @pl.when(step == 0)
    def _():
        start = 0
        for ref in cols:
            high, low = split(ref[...])
            high_cols[start : start + ref.shape[0], :] = high
            low_cols[start : start + ref.shape[0], :] = low
            start += ref.shape[0]
        size = rows.shape[1]
        for i in range(4):
            high, low = split(rows[order[i]])
            high_rows[i * size : (i + 1) * size, :] = high
            low_rows[i * size : (i + 1) * size, :] = low

    width = high_out.shape[1]
    here = pl.ds(pl.multiple_of(step * width, width), width)
    cols_here = (high_cols[here, :], low_cols[here, :])
    size = high_out.shape[0] // 4
    for i in range(4):
        rows_here = slice(i * size, (i + 1) * size)
        inner = dot_split(
            (high_rows[rows_here, :], low_rows[rows_here, :]),
            cols_here,
            (((1,), (1,)), ((), ())),
        )
        high, low = split(inner + inner * inner * inner)
        high_out[rows_here, :] = high
        low_out[rows_here, :] = low


def whole(part):
    return pl.BlockSpec(part.shape, lambda i, *_: (0,) * part.ndim)


def form(order, rows, cols, block):
    width = sum(part.shape[0] for part in cols)
    total, depth = 4 * rows.shape[1], rows.shape[2]
    tile = pl.BlockSpec((total, block), lambda i, *_: (0, i))
    return pl.pallas_call(
        lambda *refs: form_kernel(len(cols), *refs),
        grid_spec=pltpu.PrefetchScalarGridSpec(
            num_scalar_prefetch=1,
            grid=(width // block,),
            in_specs=[whole(part) for part in [*cols, rows]],
            out_specs=[tile, tile],
            scratch_shapes=[pltpu.VMEM((width, depth), BF16)] * 2
            + [pltpu.VMEM((total, depth), BF16)] * 2,
        ),
        out_shape=[jax.ShapeDtypeStruct((total, width), BF16)] * 2,
        cost_estimate=pl.CostEstimate(
            flops=6 * total * width * depth, bytes_accessed=4 * total * width, transcendentals=0
        ),
        name="form",
    )(order, *cols, rows)


def apply_kernel(n, add, order, values, *refs):
    if add:
        before, refs = refs[0], refs[1:]
    tests, high_tile, low_tile, out, sums = refs[:n], *refs[n:]
    step = pl.program_id(0)
    count = high_tile.shape[1] // values.shape[1]
    part = jnp.concatenate([values[order[step * count + i]] for i in range(count)], axis=0)
    result = dot_split((high_tile[...], low_tile[...]), split(part))

    @pl.when(step == 0)
    def _():
        out[...] = result + before[...] if add else result

    @pl.when(step > 0)
    def _():
        out[...] += result

    @pl.when(step == pl.num_programs(0) - 1)
    def _():
        sums[...] = jnp.zeros_like(sums)
        for j, test in enumerate(tests):
            size, block = test.shape[0] // 4, out.shape[0] // 4
            for i in range(4):
                product = test[i * size : (i + 1) * size, :] * out[i * block : i * block + size, :]
                sums[j : j + 1, :] += jnp.sum(product, axis=0, keepdims=True)


def apply(tile, block, order, values, tests=(), before=None, start=0):
    total, columns = tile[0].shape[0], values.shape[2]
    width = order.shape[0] * values.shape[1]
    tiles = pl.BlockSpec((total, block), lambda i, *_: (0, start // block + i))
    operands = [values] + ([] if before is None else [before]) + list(tests)
    out_shape = [
        jax.ShapeDtypeStruct((total, columns), F32),
        jax.ShapeDtypeStruct((8, columns), F32),
    ]
    return pl.pallas_call(
        lambda *refs: apply_kernel(len(tests), before is not None, *refs),
        grid_spec=pltpu.PrefetchScalarGridSpec(
            num_scalar_prefetch=1,
            grid=(width // block,),
            in_specs=[whole(part) for part in operands] + [tiles, tiles],
            out_specs=[whole(part) for part in out_shape],
        ),
        out_shape=out_shape,
        cost_estimate=pl.CostEstimate(
            flops=6 * total * width * columns, bytes_accessed=4 * total * width, transcendentals=0
        ),
        name="apply",
    )(order, *operands, *tile)


def total_sums(partial, samples):
    devices = lax.axis_size("row") * lax.axis_size("col")
    spread = jnp.broadcast_to(partial[None], (devices,) + partial.shape)
    sums = jnp.sum(lax.all_to_all(spread, AXES, 0, 0), axis=0)
    return jnp.sum(sums.reshape(partial.shape[0], samples, -1), axis=2)


def shards(
    features,
    new_features,
    lengths,
    targets,
    prior_train,
    noise_draw,
    prior_new,
    time_kernel,
    noise_var,
):
    checkpoints = time_kernel.shape[0]
    columns = prior_train.shape[1]
    samples = columns // checkpoints
    items = features.shape[0]
    block = items + new_features.shape[0]

    both = jnp.concatenate([features, new_features], axis=0)
    normed = both / jnp.sqrt(jnp.sum(both * both, axis=1, keepdims=True) + 1e-06)

    line = lax.axis_size("col")
    rows = lax.all_to_all(jnp.broadcast_to(normed[None], (line,) + normed.shape), "col", 0, 0)
    cols = [part for half in plane_gather(normed[:items]) for part in half]
    middle = block // 2

    mixing = jnp.kron(jnp.eye(samples, dtype=F32), time_kernel)

    def mix(values):
        return jnp.dot(values, mixing, precision=lax.Precision.HIGHEST)

    position = jnp.arange(columns, dtype=jnp.int32) % checkpoints
    mask = (position[None, :] < lengths[:, None]).astype(F32)
    noise_cols = jnp.tile(noise_var, samples)
    rhs = mask * (jnp.tile(targets, (1, samples)) - prior_train - jnp.sqrt(noise_cols) * noise_draw)
    plane = lax.axis_size("row")
    order = plane_order()
    half = items // 2

    def exchange(values):
        spread_out = jnp.broadcast_to(values[None], (plane,) + values.shape)
        received = lax.all_to_all(spread_out, "row", 0, 0)
        return received.reshape(-1, half, columns)

    def line_gather(values):
        own = join(ring(values, "dz"))
        return own, shift(own, core=1)

    def reduce_rows(own, other):
        received = shift(other, core=1)
        own, below, above, opposite = jnp.split(own + received, 4)
        up = shift(opposite[:middle], dz=1)
        down = shift(opposite[middle:], dz=-1)
        above = jnp.concatenate([above[:middle] + up, above[middle:]], axis=0)
        below = jnp.concatenate([below[:middle], below[middle:] + down], axis=0)
        own = own + (shift(above, dz=1) + shift(below, dz=-1))
        return own[:items], own[items:]

    def spread(scalars):
        return jnp.repeat(scalars, checkpoints)[None, :]

    def local_sums(*pairs):
        return [jnp.sum(first * second, axis=0) for first, second in pairs]

    mixed = exchange(mix(rhs))
    rhs_own, rhs_other = line_gather(rhs)
    tile_other = form(line_order(1), rows, cols, 512)
    tile_own = form(line_order(0), rows, cols, 512)
    other, sums_other = apply(tile_other, 512, order, mixed, [rhs_other])
    own, sums_own = apply(tile_own, 512, order, mixed, [rhs_own])
    norm_first, noise_first = local_sums((rhs, rhs), (rhs, noise_cols * rhs))
    curve_first = sums_own[0] + sums_other[0] + noise_first
    norm_first, curve_first = total_sums(jnp.stack([norm_first, curve_first]), samples)
    train, new_first = reduce_rows(own, other)
    image = mask * train + noise_cols * rhs
    step_first = norm_first / curve_first
    residual = rhs - spread(step_first) * image

    start = mix(residual)
    mixed = [exchange(start[:half]), exchange(start[half:])]
    res_own, res_other = line_gather(residual)

    def second(tile, tests):
        orders = order.reshape(2, -1) // 2
        width = items * plane // 2
        result, _ = apply(tile, 512, orders[0], mixed[0])
        return apply(tile, 512, orders[1], mixed[1], tests, result, width)

    other, sums_other = second(tile_other, [rhs_other, res_other])
    own, sums_own = second(tile_own, [rhs_own, res_own])
    tests = sums_own + sums_other
    norm_next, res_image, noise_rhs, noise_res = local_sums(
        (residual, residual),
        (residual, image),
        (rhs, noise_cols * residual),
        (residual, noise_cols * residual),
    )
    partial = jnp.stack([norm_next, res_image, tests[0] + noise_rhs, tests[1] + noise_res])
    norm_next, res_image, rhs_answer, res_answer = total_sums(partial, samples)
    ratio = norm_next / norm_first
    curve_second = res_answer + ratio * (res_image + rhs_answer + ratio * curve_first)
    step_second = norm_next / curve_second
    train, new_second = reduce_rows(own, other)
    answer = mask * train + noise_cols * residual
    residual = residual - spread(step_second) * (answer + spread(ratio) * image)
    predicted = (
        prior_new
        + spread(step_first + step_second * ratio) * new_first
        + spread(step_second) * new_second
    )
    return (residual, predicted)


def solution(mesh):
    return jax.shard_map(
        shards,
        mesh=mesh,
        in_specs=(
            P(("row", "col"), None),
            P(("row", "col"), None),
            P(("row", "col")),
            P(("row", "col"), None),
            P(("row", "col"), None),
            P(("row", "col"), None),
            P(("row", "col"), None),
            P(),
            P(),
        ),
        out_specs=(P(("row", "col"), None), P(("row", "col"), None)),
        check_vma=False,
    )
```

```python
import jax
import jax.numpy as jnp
import numpy as np
from jax import lax
from jax.experimental import pallas as pl
from jax.experimental.pallas import tpu as pltpu
from jax.sharding import PartitionSpec as P


AXES = ("row", "col")
F32 = jnp.float32
BF16 = jnp.bfloat16


def index(x, y, z, core):
    return ((x % 4) * 4 + y % 4) * 8 + (z % 4) * 2 + core % 2


def shift(values, dx=0, dy=0, dz=0, core=0):
    pairs = [
        (index(x, y, z, k), index(x + dx, y + dy, z + dz, k + core))
        for x in range(4)
        for y in range(4)
        for z in range(4)
        for k in range(2)
    ]
    return lax.ppermute(values, AXES, pairs)


def ring(values, axis):
    half = values.shape[0] // 2
    below = shift(values, **{axis: 1})
    above = shift(values, **{axis: -1})
    first = shift(below[:half], **{axis: 1})
    second = shift(above[half:], **{axis: -1})
    return [values, below, above, first, second]


def join_kernel(*refs):
    start = 0
    for ref in refs[:-1]:
        refs[-1][start : start + ref.shape[0], :] = ref[...]
        start += ref.shape[0]


def join(parts):
    rows = sum(part.shape[0] for part in parts)
    return pl.pallas_call(
        join_kernel,
        out_shape=jax.ShapeDtypeStruct((rows, parts[0].shape[1]), F32),
        name="join",
    )(*parts)


def plane_half(values, near, far):
    return ring(join(ring(values, near)), far)


def plane_gather(values):
    middle = values.shape[0] // 2
    return [plane_half(values[:middle], "dx", "dy"), plane_half(values[middle:], "dy", "dx")]


OFFSETS = (0, -1, 1, 2)


def at(table, axis):
    return lax.dynamic_index_in_dim(jnp.asarray(table), lax.axis_index(axis), keepdims=False)


def plane_order():
    steps = [(near, far) for far in OFFSETS for near in OFFSETS]
    table = []
    for x in range(4):
        for y in range(4):
            one = [((x + near) % 4 * 4 + (y + far) % 4) * 2 for near, far in steps]
            two = [((x + far) % 4 * 4 + (y + near) % 4) * 2 + 1 for near, far in steps]
            table.append(one + two)
    return at(np.array(table, np.int32), "row")


def line_order(other):
    table = [
        [(z + step) % 4 * 2 + (core + other) % 2 for step in OFFSETS]
        for z in range(4)
        for core in range(2)
    ]
    return at(np.array(table, np.int32), "col")


def split(values):
    high = values.astype(BF16)
    return high, (values - high.astype(F32)).astype(BF16)


def dot(first, second, dims=(((1,), (0,)), ((), ()))):
    return lax.dot_general(first, second, dims, preferred_element_type=F32)


def dot_split(first, second, dims=(((1,), (0,)), ((), ()))):
    return dot(first[0], second[0], dims) + (
        dot(first[0], second[1], dims) + dot(first[1], second[0], dims)
    )


def form_kernel(n, order, *refs):
    cols, rows, high_out, low_out, high_cols, low_cols, high_rows, low_rows = refs[:n], *refs[n:]
    step = pl.program_id(0)

    @pl.when(step == 0)
    def _():
        start = 0
        for ref in cols:
            high, low = split(ref[...])
            high_cols[start : start + ref.shape[0], :] = high
            low_cols[start : start + ref.shape[0], :] = low
            start += ref.shape[0]
        size = rows.shape[1]
        for i in range(4):
            high, low = split(rows[order[i]])
            high_rows[i * size : (i + 1) * size, :] = high
            low_rows[i * size : (i + 1) * size, :] = low

    width = high_out.shape[1]
    here = pl.ds(pl.multiple_of(step * width, width), width)
    cols_here = (high_cols[here, :], low_cols[here, :])
    size = high_out.shape[0] // 4
    for i in range(4):
        rows_here = slice(i * size, (i + 1) * size)
        inner = dot_split(
            (high_rows[rows_here, :], low_rows[rows_here, :]),
            cols_here,
            (((1,), (1,)), ((), ())),
        )
        high, low = split(inner + inner * inner * inner)
        high_out[rows_here, :] = high
        low_out[rows_here, :] = low


def whole(part):
    return pl.BlockSpec(part.shape, lambda i, *_: (0,) * part.ndim)


def form(order, rows, cols, block):
    width = sum(part.shape[0] for part in cols)
    total, depth = 4 * rows.shape[1], rows.shape[2]
    tile = pl.BlockSpec((total, block), lambda i, *_: (0, i))
    return pl.pallas_call(
        lambda *refs: form_kernel(len(cols), *refs),
        grid_spec=pltpu.PrefetchScalarGridSpec(
            num_scalar_prefetch=1,
            grid=(width // block,),
            in_specs=[whole(part) for part in [*cols, rows]],
            out_specs=[tile, tile],
            scratch_shapes=[pltpu.VMEM((width, depth), BF16)] * 2
            + [pltpu.VMEM((total, depth), BF16)] * 2,
        ),
        out_shape=[jax.ShapeDtypeStruct((total, width), BF16)] * 2,
        cost_estimate=pl.CostEstimate(
            flops=6 * total * width * depth, bytes_accessed=4 * total * width, transcendentals=0
        ),
        name="form",
    )(order, *cols, rows)


def apply_kernel(n, add, order, values, *refs):
    if add:
        before, refs = refs[0], refs[1:]
    tests, high_tile, low_tile, out, sums = refs[:n], *refs[n:]
    step = pl.program_id(0)
    count = high_tile.shape[1] // values.shape[1]
    part = jnp.concatenate([values[order[step * count + i]] for i in range(count)], axis=0)
    result = dot_split((high_tile[...], low_tile[...]), split(part))

    @pl.when(step == 0)
    def _():
        out[...] = result + before[...] if add else result

    @pl.when(step > 0)
    def _():
        out[...] += result

    @pl.when(step == pl.num_programs(0) - 1)
    def _():
        sums[...] = jnp.zeros_like(sums)
        for j, test in enumerate(tests):
            size, block = test.shape[0] // 4, out.shape[0] // 4
            for i in range(4):
                product = test[i * size : (i + 1) * size, :] * out[i * block : i * block + size, :]
                sums[j : j + 1, :] += jnp.sum(product, axis=0, keepdims=True)


def apply(tile, block, order, values, tests=(), before=None, start=0):
    total, columns = tile[0].shape[0], values.shape[2]
    width = order.shape[0] * values.shape[1]
    tiles = pl.BlockSpec((total, block), lambda i, *_: (0, start // block + i))
    operands = [values] + ([] if before is None else [before]) + list(tests)
    out_shape = [
        jax.ShapeDtypeStruct((total, columns), F32),
        jax.ShapeDtypeStruct((8, columns), F32),
    ]
    return pl.pallas_call(
        lambda *refs: apply_kernel(len(tests), before is not None, *refs),
        grid_spec=pltpu.PrefetchScalarGridSpec(
            num_scalar_prefetch=1,
            grid=(width // block,),
            in_specs=[whole(part) for part in operands] + [tiles, tiles],
            out_specs=[whole(part) for part in out_shape],
        ),
        out_shape=out_shape,
        cost_estimate=pl.CostEstimate(
            flops=6 * total * width * columns, bytes_accessed=4 * total * width, transcendentals=0
        ),
        name="apply",
    )(order, *operands, *tile)


def total_sums(partial, samples):
    devices = lax.axis_size("row") * lax.axis_size("col")
    spread = jnp.broadcast_to(partial[None], (devices,) + partial.shape)
    sums = jnp.sum(lax.all_to_all(spread, AXES, 0, 0), axis=0)
    return jnp.sum(sums.reshape(partial.shape[0], samples, -1), axis=2)


def shards(
    features,
    new_features,
    lengths,
    targets,
    prior_train,
    noise_draw,
    prior_new,
    time_kernel,
    noise_var,
):
    checkpoints = time_kernel.shape[0]
    columns = prior_train.shape[1]
    samples = columns // checkpoints
    items = features.shape[0]
    block = items + new_features.shape[0]

    both = jnp.concatenate([features, new_features], axis=0)
    normed = both / jnp.sqrt(jnp.sum(both * both, axis=1, keepdims=True) + 1e-06)

    line = lax.axis_size("col")
    rows = lax.all_to_all(jnp.broadcast_to(normed[None], (line,) + normed.shape), "col", 0, 0)
    cols = [part for half in plane_gather(normed[:items]) for part in half]
    middle = block // 2

    mixing = jnp.kron(jnp.eye(samples, dtype=F32), time_kernel)

    def mix(values):
        return jnp.dot(values, mixing, precision=lax.Precision.HIGH)

    position = jnp.arange(columns, dtype=jnp.int32) % checkpoints
    mask = (position[None, :] < lengths[:, None]).astype(F32)
    noise_cols = jnp.tile(noise_var, samples)
    rhs = mask * (jnp.tile(targets, (1, samples)) - prior_train - jnp.sqrt(noise_cols) * noise_draw)
    plane = lax.axis_size("row")
    order = plane_order()
    half = items // 2

    def exchange(values):
        spread_out = jnp.broadcast_to(values[None], (plane,) + values.shape)
        received = lax.all_to_all(spread_out, "row", 0, 0)
        return received.reshape(-1, half, columns)

    def line_gather(values):
        own = join(ring(values, "dz"))
        return own, shift(own, core=1)

    def reduce_rows(own, other):
        received = shift(other, core=1)
        own, below, above, opposite = jnp.split(own + received, 4)
        up = shift(opposite[:middle], dz=1)
        down = shift(opposite[middle:], dz=-1)
        above = jnp.concatenate([above[:middle] + up, above[middle:]], axis=0)
        below = jnp.concatenate([below[:middle], below[middle:] + down], axis=0)
        own = own + (shift(above, dz=1) + shift(below, dz=-1))
        return own[:items], own[items:]

    def spread(scalars):
        return jnp.repeat(scalars, checkpoints)[None, :]

    def local_sums(*pairs):
        return [jnp.sum(first * second, axis=0) for first, second in pairs]

    mixed = exchange(mix(rhs))
    rhs_own, rhs_other = line_gather(rhs)
    tile_other = form(line_order(1), rows, cols, 512)
    tile_own = form(line_order(0), rows, cols, 512)
    other, sums_other = apply(tile_other, 1024, order, mixed, [rhs_other])
    own, sums_own = apply(tile_own, 512, order, mixed, [rhs_own])
    norm_first, noise_first = local_sums((rhs, rhs), (rhs, noise_cols * rhs))
    curve_first = sums_own[0] + sums_other[0] + noise_first
    norm_first, curve_first = total_sums(jnp.stack([norm_first, curve_first]), samples)
    train, new_first = reduce_rows(own, other)
    image = mask * train + noise_cols * rhs
    step_first = norm_first / curve_first
    residual = rhs - spread(step_first) * image

    start = mix(residual)
    mixed = [exchange(start[:half]), exchange(start[half:])]
    res_own, res_other = line_gather(residual)

    def second(tile, tests):
        orders = order.reshape(2, -1) // 2
        width = items * plane // 2
        result, _ = apply(tile, 256, orders[0], mixed[0])
        return apply(tile, 512, orders[1], mixed[1], tests, result, width)

    other, sums_other = second(tile_other, [rhs_other, res_other])
    own, sums_own = second(tile_own, [rhs_own, res_own])
    tests = sums_own + sums_other
    norm_next, res_image, noise_rhs, noise_res = local_sums(
        (residual, residual),
        (residual, image),
        (rhs, noise_cols * residual),
        (residual, noise_cols * residual),
    )
    partial = jnp.stack([norm_next, res_image, tests[0] + noise_rhs, tests[1] + noise_res])
    norm_next, res_image, rhs_answer, res_answer = total_sums(partial, samples)
    ratio = norm_next / norm_first
    curve_second = res_answer + ratio * (res_image + rhs_answer + ratio * curve_first)
    step_second = norm_next / curve_second
    train, new_second = reduce_rows(own, other)
    answer = mask * train + noise_cols * residual
    residual = residual - spread(step_second) * (answer + spread(ratio) * image)
    predicted = (
        prior_new
        + spread(step_first + step_second * ratio) * new_first
        + spread(step_second) * new_second
    )
    return (residual, predicted)


def solution(mesh):
    return jax.shard_map(
        shards,
        mesh=mesh,
        in_specs=(
            P(("row", "col"), None),
            P(("row", "col"), None),
            P(("row", "col")),
            P(("row", "col"), None),
            P(("row", "col"), None),
            P(("row", "col"), None),
            P(("row", "col"), None),
            P(),
            P(),
        ),
        out_specs=(P(("row", "col"), None), P(("row", "col"), None)),
        check_vma=False,
    )
```
